256 devices in a mesh: pipe: 16 (over y, x), dp: 16 (over z, core).
Axes of the slice: x: 4, y: 4, z: 8, core: 2. Of those that a mesh axis runs over, the one named last changes fastest.
Arguments:
- first_input: bfloat16 [4, 1024, 8192], P(None, 'dp'), may hold values from -6 to 6
- section_gain: float32 [16, 8192], P('pipe'), may hold values from 0.5 to 1.5
- value_panel: bfloat16 [16, 8192, 512], P('pipe', 'dp'), may hold values from -0.0625 to 0.0625
- output_panel: bfloat16 [16, 512, 8192], P('pipe', 'dp'), may hold values from -0.125 to 0.125
- value_tiles: bfloat16 [16, 32, 4096], P('pipe', 'dp'), may hold values from -0.1875 to 0.1875
- output_tiles: bfloat16 [16, 32, 4096], P('pipe', 'dp'), may hold values from -0.375 to 0.375
- value_blocks: int32 [16, 32], P('pipe'), may hold values from 0 to 1023, as said below
- output_blocks: int32 [16, 32], P('pipe'), may hold values from 0 to 1023, as said below
- upstream: bfloat16 [16, 4, 1024, 8192], P('pipe', None, 'dp'), may hold values from -0.08984375 to 0.08984375
Outputs:
- value_tile_grads: float32 [16, 32, 4096], P('pipe', 'dp')
- output_tile_grads: float32 [16, 32, 4096], P('pipe', 'dp')
The draws below stay inside these ranges and needn't reach their ends.
Inputs may be any that keep to these rules, and one draw needn't show every extreme that they name: `value_blocks`: the 32 block numbers of one section and one matrix are distinct; in section 0 both 0 and the largest block number occur. `output_blocks`: the 32 block numbers of one section and one matrix are distinct; in section 0 both 0 and the largest block number occur.
All inputs are finite; a program needn't handle non-finite values.
Results may differ from the reference program's by a relative error of at most 0.025.
Values may be sent and summed in bfloat16 or wider, within the bound.
A program may use at most 192 MiB of HBM per device.

```python
import jax
import jax.numpy as jnp
from jax import lax

D = 8192
KVW = 512
BLK = 64
TILES = 32
MICRO = 4
SEGMENTS = 16
TOKENS = 1024


def pick_blocks(key, block_count):
    subkeys = jax.random.split(key, SEGMENTS)
    ranking = jax.vmap(lambda subkey: jax.random.permutation(subkey, block_count))(subkeys)
    ranking = ranking.astype(jnp.int32)
    ranking = ranking.at[0, 0].set(-2).at[0, block_count - 1].set(-1)
    return jnp.argsort(ranking, axis=1, stable=True)[:, :TILES].astype(jnp.int32)


def draw_value_blocks(key, part):
    return pick_blocks(jax.random.fold_in(key, 11), D // BLK * (KVW // BLK))


def draw_output_blocks(key, part):
    return pick_blocks(jax.random.fold_in(key, 23), D // BLK * (KVW // BLK))


def levels(own_key, extent, cuts, smallest, largest):
    def one(position, shards_of):
        steps = jax.random.uniform(jax.random.fold_in(jax.random.fold_in(own_key, 6), position), (shards_of,), jnp.float32, smallest / len(cuts), largest / len(cuts))
        return jnp.repeat(jnp.exp(steps), extent[position] // shards_of).reshape((-1,) + (1,) * (len(extent) - position - 1))

    loudness = one(*cuts[0])
    for cut in cuts[1:]:
        loudness = loudness * one(*cut)
    return loudness


def scatter_about(stream_key, shape, deviation, bound, pieces=(), kind=jnp.bfloat16):
    drawn = jax.random.normal(stream_key, shape, jnp.float32) * deviation
    if len(pieces) > 0:
        drawn = levels(stream_key, shape, pieces, -0.22, 0.18) * drawn
    return jnp.clip(drawn, min=-bound, max=bound).astype(kind)


def setup_inputs(seed: int = 0) -> dict:
    key_of = jax.random.split(jax.random.key(seed), 10)
    return {
        "first_input": scatter_about(key_of[0], (MICRO, TOKENS, D), 1.0, 6.0, ((1, 16),)),
        "section_gain": jnp.clip(0.5 + 1.0 * jax.random.uniform(key_of[1], (SEGMENTS, D), jnp.float32) ** levels(key_of[1], (SEGMENTS, D), ((0, 16),), -0.2, 0.2), 0.5, 1.5),
        "value_panel": scatter_about(key_of[2], (SEGMENTS, D, KVW), D ** -0.5, 0.0625, ((0, 16), (1, 16))),
        "output_panel": scatter_about(key_of[3], (SEGMENTS, KVW, D), (4 * KVW) ** -0.5, 0.125, ((0, 16), (1, 16))),
        "value_tiles": scatter_about(key_of[4], (SEGMENTS, TILES, BLK * BLK), (D // 8) ** -0.5, 0.1875, ((0, 16), (1, 16))),
        "output_tiles": scatter_about(key_of[5], (SEGMENTS, TILES, BLK * BLK), (KVW // 2) ** -0.5, 0.375, ((0, 16), (1, 16))),
        "value_blocks": draw_value_blocks(jax.random.fold_in(key_of[9], 71), 0),
        "output_blocks": draw_output_blocks(jax.random.fold_in(key_of[9], 71), 0),
        "upstream": scatter_about(key_of[8], (SEGMENTS, MICRO, TOKENS, D), 0.015, 0.08984375, ((0, 16), (2, 16))),
    }


NORM_EPS = 1e-05

def effective_panel(panel, delta, blocks):
    col_count = panel.shape[1] // BLK
    blocked = panel.reshape(panel.shape[0] // BLK, BLK, col_count, BLK)
    blocked = blocked.at[blocks // col_count, :, blocks % col_count, :].add(delta.reshape(blocks.shape[0], BLK, BLK))
    return blocked.reshape(panel.shape)

def section_forward(hidden, scaling, value_eff, output_eff):
    widened = hidden.astype(jnp.float32)
    inverse_rms = lax.rsqrt(lax.optimization_barrier(jnp.mean(widened * widened, axis=-1, keepdims=True)) + NORM_EPS)
    normed = (widened * inverse_rms * scaling).astype(jnp.bfloat16)
    values = jnp.dot(normed, value_eff, preferred_element_type=jnp.float32).astype(jnp.bfloat16)
    mixed = jnp.dot(values, output_eff, preferred_element_type=jnp.float32)
    following = (widened + mixed).astype(jnp.bfloat16)
    return (normed, values, following)

def tile_products(acts, grads, blocks, col_count):
    count = acts.shape[0]
    left_blocks = acts.reshape(count, acts.shape[1] // BLK, BLK)[:, blocks // col_count, :].astype(jnp.float32)
    right_blocks = grads.reshape(count, grads.shape[1] // BLK, BLK)[:, blocks % col_count, :].astype(jnp.float32)
    products = jnp.einsum('nka,nkb->kab', left_blocks, right_blocks)
    return products.reshape(blocks.shape[0], BLK * BLK)

def reference(first_input, section_gain, value_panel, output_panel, value_tiles, output_tiles, value_blocks, output_blocks, upstream):
    hidden = first_input.reshape(MICRO * TOKENS, D)
    value_list = []
    output_list = []
    for section in range(SEGMENTS):
        value_eff = effective_panel(value_panel[section], value_tiles[section], value_blocks[section])
        output_eff = effective_panel(output_panel[section], output_tiles[section], output_blocks[section])
        normed, values, following = section_forward(hidden, section_gain[section], value_eff, output_eff)
        incoming = upstream[section].reshape(MICRO * TOKENS, D)
        value_back = lax.dot_general(incoming, output_eff, (((1,), (1,)), ((), ())), preferred_element_type=jnp.float32).astype(jnp.bfloat16)
        value_list.append(tile_products(normed, value_back, value_blocks[section], KVW // BLK))
        output_list.append(tile_products(values, incoming, output_blocks[section], D // BLK))
        hidden = following
    return (jnp.stack(value_list), jnp.stack(output_list))
```

```python
import functools

import jax
import jax.numpy as jnp
from jax import lax
from jax.experimental import pallas as pl
from jax.experimental.pallas import tpu as pltpu
from jax.sharding import PartitionSpec as P

BLK = 64
EPS = 1e-05
CHUNK = 16
WIDE = 512
MESH = pl.DeviceIdType.MESH


def meet(peers):
    barrier = pltpu.get_barrier_semaphore()
    for peer in peers:
        pl.semaphore_signal(barrier, inc=1, device_id=peer, device_id_type=MESH)
    pl.semaphore_wait(barrier, len(peers))


def share_tiles(dp_count, own_ref, all_ref, send_sems, recv_sems, own_sem):
    stage = lax.axis_index("pipe")
    me = lax.axis_index("dp")

    def peer(offset):
        return (stage, lax.rem(me + offset, dp_count))

    meet([peer(offset) for offset in range(1, dp_count)])

    def copy(offset):
        return pltpu.make_async_remote_copy(
            src_ref=own_ref,
            dst_ref=all_ref.at[me],
            send_sem=send_sems.at[offset],
            recv_sem=recv_sems.at[offset],
            device_id=peer(offset),
            device_id_type=MESH,
        )

    own = pltpu.make_async_copy(own_ref, all_ref.at[me], own_sem)
    own.start()
    copies = [copy(offset) for offset in range(1, dp_count)]
    for each in copies:
        each.start()
    own.wait()
    for each in copies:
        each.wait()


def chain(
    dp_count,
    pipe_count,
    value_in,
    output_in,
    first_in,
    gain_ref,
    upstream_ref,
    hidden_out,
    inverse,
    values_ref,
    back_ref,
    value_all,
    output_all,
    inbox,
    outbox,
    back_sum,
    ring_send,
    ring_recv,
    pair_send,
    pair_recv,
    hop_send,
    hop_recv,
    first_sem,
    keep_sem,
):
    stage = lax.axis_index("pipe")
    me = lax.axis_index("dp")
    ring = dp_count // 2
    half = ring // 2
    place = me // 2
    core = lax.rem(me, 2)
    value_rows = value_in.shape[0]
    output_rows = output_in.shape[0]
    width = output_in.shape[1]
    value_width = value_in.shape[1]
    chunk_count = inbox.shape[0]
    tokens = chunk_count * CHUNK
    wide_count = width // WIDE

    following = (lax.rem(stage + 1, pipe_count), me)
    previous = (lax.rem(stage + pipe_count - 1, pipe_count), me)
    near = [(stage, lax.rem(place + step, ring) * 2 + core) for step in (1, ring - 1)]
    meet(near + [(stage, place * 2 + 1 - core), following, previous])

    load_first = pltpu.make_async_copy(first_in, inbox, first_sem)

    @pl.when(stage == 0)
    def _():
        load_first.start()

    def slot(kind, index):
        if kind == 0:
            return value_all.at[pl.ds(pl.multiple_of(index * value_rows, value_rows), value_rows), :]
        return output_all.at[pl.ds(pl.multiple_of(index * output_rows, output_rows), output_rows), :]

    def at_distance(way, distance):
        step = -distance if way == 0 else distance
        return lax.rem(place + step + ring, ring) * 2 + core

    def ring_copy(way, kind, distance):
        index = at_distance(way, distance)
        source = slot(kind, index)
        if distance == 0:
            source = value_in if kind == 0 else output_in
        goal = lax.rem(place + (1 if way == 0 else ring - 1), ring) * 2 + core
        return pltpu.make_async_remote_copy(
            src_ref=source,
            dst_ref=slot(kind, index),
            send_sem=ring_send.at[way, kind, distance],
            recv_sem=ring_recv.at[way, kind, distance],
            device_id=(stage, goal),
            device_id_type=MESH,
        )

    def ring_arrival(way, kind, distance):
        index = at_distance(way, distance)
        return pltpu.make_async_remote_copy(
            src_ref=slot(kind, index),
            dst_ref=slot(kind, index),
            send_sem=ring_send.at[way, kind, distance - 1],
            recv_sem=ring_recv.at[way, kind, distance - 1],
            device_id=(stage, place * 2 + core),
            device_id_type=MESH,
        )

    def pair_copy(number, way, kind, distance):
        index = at_distance(way, distance)
        source = slot(kind, index)
        if distance == 0:
            source = value_in if kind == 0 else output_in
        return pltpu.make_async_remote_copy(
            src_ref=source,
            dst_ref=slot(kind, index),
            send_sem=pair_send.at[number],
            recv_sem=pair_recv.at[number],
            device_id=(stage, place * 2 + 1 - core),
            device_id_type=MESH,
        )

    def pair_arrival(number, way, kind, distance):
        step = -distance if way == 0 else distance
        index = lax.rem(place + step + ring, ring) * 2 + 1 - core
        return pltpu.make_async_remote_copy(
            src_ref=slot(kind, index),
            dst_ref=slot(kind, index),
            send_sem=pair_send.at[number],
            recv_sem=pair_recv.at[number],
            device_id=(stage, place * 2 + 1 - core),
            device_id_type=MESH,
        )

    def reach(way, kind):
        return half if way == kind else half - 1

    sent = []
    pairs = []
    arrivals = []

    def pass_on(way, kind, distance):
        number = len(pairs)
        copy = pair_copy(number, way, kind, distance)
        copy.start()
        pairs.append(copy)
        arrivals.append(pair_arrival(number, way, kind, distance))

    def send_on(way, kind, distance):
        if distance < reach(way, kind):
            copy = ring_copy(way, kind, distance)
            copy.start()
            sent.append(copy)

    for kind in (0, 1):
        for way in (0, 1):
            send_on(way, kind, 0)
    for kind in (0, 1):
        pass_on(0, kind, 0)
    value_all[pl.ds(pl.multiple_of(me * value_rows, value_rows), value_rows), :] = value_in[...]
    output_all[pl.ds(pl.multiple_of(me * output_rows, output_rows), output_rows), :] = output_in[...]
    for distance in range(1, half + 1):
        for kind in (0, 1):
            for way in (0, 1):
                if distance <= reach(way, kind):
                    ring_arrival(way, kind, distance).wait_recv()
                    send_on(way, kind, distance)
                    pass_on(way, kind, distance)
    for arrival in arrivals:
        arrival.wait_recv()

    def back_values():
        back_sum[...] = jnp.zeros_like(back_sum)

        @pl.loop(0, wide_count)
        def _(block):
            columns = pl.ds(pl.multiple_of(block * WIDE, WIDE), WIDE)
            back_sum[...] += lax.dot_general(
                upstream_ref[:, columns],
                output_all[:, columns],
                (((1,), (1,)), ((), ())),
                preferred_element_type=jnp.float32,
            )

        back_ref[...] = back_sum[...].astype(jnp.bfloat16)

    @pl.when(stage * 2 >= pipe_count)
    def _():
        back_values()

    @pl.when(stage == 0)
    def _():
        load_first.wait()

    def hop(index):
        return pltpu.make_async_remote_copy(
            src_ref=outbox.at[index],
            dst_ref=inbox.at[index],
            send_sem=hop_send.at[index],
            recv_sem=hop_recv.at[index],
            device_id=following,
            device_id_type=MESH,
        )

    @pl.loop(0, chunk_count)
    def _(index):
        @pl.when(stage > 0)
        def _():
            hop(index).wait_recv()

        squares = jnp.zeros((CHUNK, WIDE), jnp.float32)
        mixed = jnp.zeros((CHUNK, value_width), jnp.float32)
        for block in range(wide_count):
            columns = slice(block * WIDE, (block + 1) * WIDE)
            hidden = inbox[index, :, columns].astype(jnp.float32)
            squares = squares + hidden * hidden
            scaled = (hidden * gain_ref[:, columns]).astype(jnp.bfloat16)
            mixed = mixed + jnp.dot(
                scaled, value_all[columns, :], preferred_element_type=jnp.float32
            )
        scale = lax.rsqrt(jnp.sum(squares, axis=1, keepdims=True) / width + EPS)
        inverse[index] = jnp.broadcast_to(scale, (CHUNK, 128))
        values = (mixed * scale).astype(jnp.bfloat16)
        values_ref[index] = values

        @pl.when(stage < pipe_count - 1)
        def _():
            for block in range(wide_count):
                columns = slice(block * WIDE, (block + 1) * WIDE)
                added = jnp.dot(values, output_all[:, columns], preferred_element_type=jnp.float32)
                outbox[index, :, columns] = (
                    inbox[index, :, columns].astype(jnp.float32) + added
                ).astype(jnp.bfloat16)
            hop(index).start()

    @pl.when(stage * 2 < pipe_count)
    def _():
        back_values()

    keep = pltpu.make_async_copy(inbox, hidden_out, keep_sem)
    keep.start()
    for copy in sent + pairs:
        copy.wait_send()

    @pl.when(stage < pipe_count - 1)
    def _():
        @pl.loop(0, chunk_count)
        def _(index):
            hop(index).wait_send()

    keep.wait()


def tile_grads(
    value_blocks,
    output_blocks,
    hidden_ref,
    inverse,
    values_ref,
    back_ref,
    gain_ref,
    upstream_ref,
    partial,
):
    tokens, value_width = back_ref.shape
    width = upstream_ref.shape[1]
    value_cols = value_width // BLK
    output_cols = width // BLK
    lanes = lax.broadcasted_iota(jnp.int32, (BLK, 2 * BLK), 1)

    def pair_of(block):
        return pl.ds(pl.multiple_of(lax.div(block, 2) * (2 * BLK), 2 * BLK), 2 * BLK)

    def quadrant(product, row, turn):
        upper = jnp.where(lax.rem(row, 2) == 0, product[:BLK], product[BLK:])
        return jnp.where(turn == 1, pltpu.roll(upper, BLK, 1), upper)

    @pl.loop(0, partial.shape[0])
    def _(owner):
        for which in range(2):
            number = value_blocks[owner * 2 + which]
            row, column = lax.div(number, value_cols), lax.rem(number, value_cols)
            left = hidden_ref[:, :, pair_of(row)].astype(jnp.float32)
            left = left * inverse[...] * gain_ref[:, pair_of(row)]
            left = left.reshape(tokens, 2 * BLK).astype(jnp.bfloat16)
            product = lax.dot_general(
                left,
                back_ref[:, pair_of(column)],
                (((0,), (0,)), ((), ())),
                preferred_element_type=jnp.float32,
            )
            value_part = quadrant(product, row, lax.rem(column, 2))
            number = output_blocks[owner * 2 + which]
            row, column = lax.div(number, output_cols), lax.rem(number, output_cols)
            product = lax.dot_general(
                values_ref[:, :, pair_of(row)].reshape(tokens, 2 * BLK),
                upstream_ref[:, pair_of(column)],
                (((0,), (0,)), ((), ())),
                preferred_element_type=jnp.float32,
            )
            output_part = quadrant(product, row, 1 - lax.rem(column, 2))
            partial[owner, which] = jnp.where(lanes < BLK, value_part, output_part).astype(
                jnp.bfloat16
            )


def scatter_sum(dp_count, partial, grads_ref, landing, send_sems, recv_sems):
    stage = lax.axis_index("pipe")
    me = lax.axis_index("dp")

    def peer(offset):
        return (stage, lax.rem(me + offset, dp_count))

    meet([peer(offset) for offset in range(1, dp_count)])

    def copy(offset):
        return pltpu.make_async_remote_copy(
            src_ref=partial.at[lax.rem(me + offset, dp_count)],
            dst_ref=landing.at[offset],
            send_sem=send_sems.at[offset],
            recv_sem=recv_sems.at[offset],
            device_id=peer(offset),
            device_id_type=MESH,
        )

    copies = [copy(offset) for offset in range(1, dp_count)]
    for each in copies:
        each.start()
    total = partial[me].astype(jnp.float32)
    for offset, each in enumerate(copies, start=1):
        each.wait_recv()
        total = total + landing[offset].astype(jnp.float32)
    grads_ref[...] = total
    for each in copies:
        each.wait_send()


def shards(
    pipe_count,
    dp_count,
    first_input,
    section_gain,
    value_panel,
    output_panel,
    value_tiles,
    output_tiles,
    value_blocks,
    output_blocks,
    upstream,
):
    width = first_input.shape[2]
    tokens = first_input.shape[0] * first_input.shape[1]
    value_width = value_panel.shape[2]
    value_rows = value_panel.shape[1]
    output_rows = output_panel.shape[1]
    tile_count = value_blocks.shape[1]
    chunk_count = tokens // CHUNK
    me = lax.axis_index("dp")
    vmem = pl.BlockSpec(memory_space=pltpu.VMEM)
    smem = pl.BlockSpec(memory_space=pltpu.SMEM)
    hbm = pl.BlockSpec(memory_space=pl.ANY)
    dma = pltpu.SemaphoreType.DMA

    own = jnp.concatenate(
        [value_tiles.reshape(BLK, 2 * BLK), output_tiles.reshape(BLK, 2 * BLK)], axis=0
    )
    shared = pl.pallas_call(
        functools.partial(share_tiles, dp_count),
        out_shape=jax.ShapeDtypeStruct((dp_count, 2 * BLK, 2 * BLK), jnp.bfloat16),
        in_specs=[vmem],
        out_specs=vmem,
        scratch_shapes=[dma((dp_count,)), dma((dp_count,)), dma(())],
        compiler_params=pltpu.CompilerParams(collective_id=0, has_side_effects=True),
        name="share_tiles",
    )(own)
    shared = shared.reshape(dp_count, 2, 2, BLK * BLK)
    value_delta = shared[:, 0].reshape(tile_count, BLK * BLK)
    output_delta = shared[:, 1].reshape(tile_count, BLK * BLK)

    value_cols = value_width // BLK
    output_cols = width // BLK
    own_rows = value_rows // BLK
    wanted = me * (own_rows * value_cols) + jnp.arange(own_rows * value_cols)
    choose = (wanted[:, None] == value_blocks[0][None, :]).astype(jnp.bfloat16)
    placed = jnp.dot(choose, value_delta, preferred_element_type=jnp.float32)
    placed = placed.reshape(own_rows, value_cols, BLK, BLK).transpose(0, 2, 1, 3)
    value_eff = (
        value_panel[0].astype(jnp.float32) + placed.reshape(value_rows, value_width)
    ).astype(jnp.bfloat16)

    start = me * output_rows
    output_delta = output_delta.reshape(tile_count, BLK // output_rows, output_rows * BLK)
    output_delta = lax.dynamic_index_in_dim(
        output_delta, lax.rem(start, BLK) // output_rows, 1, keepdims=False
    )
    wanted = start // BLK * output_cols + jnp.arange(output_cols)
    choose = (wanted[:, None] == output_blocks[0][None, :]).astype(jnp.bfloat16)
    placed = jnp.dot(choose, output_delta, preferred_element_type=jnp.float32)
    placed = placed.reshape(output_cols, output_rows, BLK).transpose(1, 0, 2)
    output_eff = (
        output_panel[0].astype(jnp.float32) + placed.reshape(output_rows, width)
    ).astype(jnp.bfloat16)

    half = dp_count // 4
    hidden_shape = (chunk_count, CHUNK, width)
    upstream = upstream.reshape(tokens, width)
    hidden, inverse, values, value_back = pl.pallas_call(
        functools.partial(chain, dp_count, pipe_count),
        out_shape=[
            jax.ShapeDtypeStruct(hidden_shape, jnp.bfloat16),
            jax.ShapeDtypeStruct((chunk_count, CHUNK, 128), jnp.float32),
            jax.ShapeDtypeStruct((chunk_count, CHUNK, value_width), jnp.bfloat16),
            jax.ShapeDtypeStruct((tokens, value_width), jnp.bfloat16),
        ],
        in_specs=[vmem, vmem, hbm, vmem, vmem],
        out_specs=[hbm, vmem, vmem, vmem],
        scratch_shapes=[
            pltpu.VMEM((width, value_width), jnp.bfloat16),
            pltpu.VMEM((value_width, width), jnp.bfloat16),
            pltpu.VMEM(hidden_shape, jnp.bfloat16),
            pltpu.VMEM(hidden_shape, jnp.bfloat16),
            pltpu.VMEM((tokens, value_width), jnp.float32),
            dma((2, 2, half)),
            dma((2, 2, half)),
            dma((dp_count,)),
            dma((dp_count,)),
            dma((chunk_count,)),
            dma((chunk_count,)),
            dma(()),
            dma(()),
        ],
        compiler_params=pltpu.CompilerParams(
            collective_id=1, has_side_effects=True, vmem_limit_bytes=60 * 1024 * 1024
        ),
        name="chain",
    )(value_eff, output_eff, first_input.reshape(hidden_shape), section_gain, upstream)
    partial = pl.pallas_call(
        tile_grads,
        out_shape=jax.ShapeDtypeStruct((dp_count, 2, BLK, 2 * BLK), jnp.bfloat16),
        in_specs=[smem, smem] + [vmem] * 6,
        out_specs=vmem,
        compiler_params=pltpu.CompilerParams(vmem_limit_bytes=32 * 1024 * 1024),
        name="tile_grads",
    )(value_blocks[0], output_blocks[0], hidden, inverse, values, value_back, section_gain, upstream)
    grads = pl.pallas_call(
        functools.partial(scatter_sum, dp_count),
        out_shape=jax.ShapeDtypeStruct((2, BLK, 2 * BLK), jnp.float32),
        in_specs=[vmem],
        out_specs=vmem,
        scratch_shapes=[
            pltpu.VMEM((dp_count, 2, BLK, 2 * BLK), jnp.bfloat16),
            dma((dp_count,)),
            dma((dp_count,)),
        ],
        compiler_params=pltpu.CompilerParams(collective_id=2, has_side_effects=True),
        name="scatter_sum",
    )(partial)
    value_grads = grads[:, :, :BLK].reshape(1, 2, BLK * BLK)
    output_grads = grads[:, :, BLK:].reshape(1, 2, BLK * BLK)
    return (value_grads, output_grads)


def solution(mesh):
    in_specs = (
        P(None, "dp", None),
        P("pipe", None),
        P("pipe", "dp", None),
        P("pipe", "dp", None),
        P("pipe", "dp", None),
        P("pipe", "dp", None),
        P("pipe", None),
        P("pipe", None),
        P("pipe", None, "dp", None),
    )
    out_specs = (P("pipe", "dp", None), P("pipe", "dp", None))
    body = functools.partial(shards, mesh.shape["pipe"], mesh.shape["dp"])
    return jax.shard_map(body, mesh=mesh, in_specs=in_specs, out_specs=out_specs, check_vma=False)
```
